256 devices in a mesh: row: 8 (over y_lo, x), col: 32 (over z, y_hi, core).
Axes of the slice: x: 4, y: 4 (y_hi: 2, y_lo: 2; y = y_hi * 2 + y_lo), z: 8, core: 2. Of those that a mesh axis runs over, the one named last changes fastest.
Arguments:
- points: float32 [32768, 128], P(('row', 'col')), may hold values from -4 to 4
- labels: int32 [32768], P(('row', 'col')), may hold values from 0 to 63
- coefficients: float32 [32768, 64], P(('row', 'col')), as said below
Outputs:
- new_coefficients: float32 [32768, 64], P(('row', 'col'))
- probabilities: float32 [32768, 64], P(('row', 'col'))
The draws below stay inside these ranges and needn't reach their ends.
Inputs may be any that keep to these rules, and one draw needn't show every extreme that they name: `coefficients`: entries have magnitude at most 300 * sqrt(32768) / 16.
All inputs are finite; a program needn't handle non-finite values.
Results may differ from the reference program's by a relative error of at most 0.012.
The reference program's roundings to bfloat16 on the way count: a program that leaves them out, or rounds other values in their place, can miss the bound.
Values may be sent and summed in bfloat16 or wider, within the bound.
No kernel may reach another device: no remote copies, remote signals or barrier semaphores. Data moves between devices by JAX's collectives and lax.ppermute only.
A program may use at most 64 MiB of HBM per device.

```python
import math
import jax
import jax.numpy as jnp
from jax import lax

FEAT = 128
CLASSES = 64
STEPS = 1
NPTS = 32768


def draw_points(key, part):
    key_basis, key_latent, key_noise = jax.random.split(jax.random.fold_in(key, 11), 3)
    sign_table = jnp.where(jax.random.bernoulli(key_basis, 0.5, (16, FEAT)), 1.0, -1.0).astype(jnp.float32) / math.sqrt(FEAT)
    spread = math.sqrt(FEAT / 8.0)
    latent = jax.random.normal(key_latent, (NPTS, 16), jnp.float32)
    noise_part = jax.random.normal(key_noise, (NPTS, FEAT), jnp.float32)
    values = spread * jnp.dot(latent, sign_table, precision=lax.Precision.HIGHEST) + 0.5 * noise_part
    return jnp.clip(values, -4.0, 4.0)


def draw_coefficients(key, part):
    values = jax.random.normal(key, (NPTS, CLASSES), jnp.float32)
    return values


def place_ends(values, stream_key, smallest, high):
    dims = values.shape
    spot = [jax.random.randint(jax.random.fold_in(stream_key, axis), (), 0, dims[axis]) for axis in range(len(dims))]
    values = values.at[tuple(spot)].set(smallest)
    longest = dims.index(max(dims))
    spot[longest] = (spot[longest] + 1) % dims[longest]
    return values.at[tuple(spot)].set(high)


def setup_inputs(seed: int = 0) -> dict:
    keys = jax.random.split(jax.random.key(seed), 4)
    return {
        "points": draw_points(jax.random.fold_in(keys[3], 71), 0),
        "labels": place_ends(jax.random.randint(keys[1], (NPTS,), 0, CLASSES), jax.random.fold_in(keys[1], 1), 0, CLASSES - 1).astype(jnp.int32),
        "coefficients": draw_coefficients(jax.random.fold_in(keys[3], 71), 0),
    }


def kernel_apply(points, current):
    squares = lax.optimization_barrier(jnp.sum(points * points, axis=1))
    block_size = math.gcd(NPTS, 2048)
    blocks = points.reshape(NPTS // block_size, block_size, FEAT)
    block_squares = squares.reshape(NPTS // block_size, block_size)
    rounded = current.astype(jnp.bfloat16)

    def one_block(pair):
        block_points, block_sq = pair
        products = lax.dot_general(block_points, points, (((1,), (1,)), ((), ())), precision=lax.Precision.HIGHEST, preferred_element_type=jnp.float32)
        distance = block_sq[:, None] + squares[None, :] - 2.0 * products
        kernel_rows = jnp.exp(-distance / FEAT).astype(jnp.bfloat16)
        return jnp.dot(kernel_rows, rounded, preferred_element_type=jnp.float32)
    result = lax.map(one_block, (blocks, block_squares))
    return result.reshape(NPTS, CLASSES)

def reference(points, labels, coefficients):
    logit_scale = 16.0 / math.sqrt(NPTS)
    onehot = (labels[:, None] == jnp.arange(CLASSES, dtype=jnp.int32)[None, :]).astype(jnp.float32)
    current = coefficients
    probabilities = jnp.zeros_like(coefficients)
    for iteration in range(STEPS):
        logits = logit_scale * kernel_apply(points, current)
        probabilities = jax.nn.softmax(logits, axis=1)
        residual = logit_scale * (probabilities - onehot)
        current = current - kernel_apply(points, residual)
    return (current, probabilities)
```

```python
import functools
import math

import jax
import jax.numpy as jnp
from jax import lax
from jax.experimental import pallas as pl
from jax.experimental.pallas import tpu as pltpu
from jax.sharding import PartitionSpec as P

FEAT = 128
CLASSES = 64
LOG2E = math.log2(math.e)
BLOCKS = 2
CHUNK = 512
BF16 = jnp.bfloat16
F32 = jnp.float32


def z_groups(cols):
    return [[z * 4 + rest for z in range(cols // 4)] for rest in range(4)]


def plane_groups(rows, cols):
    return [
        [row * cols + z * 4 + y_hi * 2 + core for row in range(rows) for y_hi in range(2)]
        for z in range(cols // 4)
        for core in range(2)
    ]


def other_core(value, cols):
    return lax.ppermute(value, "col", [(col, col ^ 1) for col in range(cols)])


def extended(block, left):
    rows = block.shape[0]
    wide = block.astype(F32)
    square = jnp.sum(wide * wide, axis=1, keepdims=True) * (-1.0 / FEAT)
    first = square.astype(BF16).astype(F32)
    rest = square - first
    second = rest.astype(BF16).astype(F32)
    third = rest - second
    lane = lax.broadcasted_iota(jnp.int32, (rows, FEAT), 1)
    at = 0 if left else 3
    ones = 3 - at
    extra = jnp.where((lane >= ones) & (lane < ones + 3), 1.0, 0.0)
    extra = jnp.where(lane == at, first, extra)
    extra = jnp.where(lane == at + 1, second, extra)
    extra = jnp.where(lane == at + 2, third, extra)
    scaled = block * jnp.asarray(2.0 / FEAT, BF16) if left else block
    return jnp.concatenate([scaled, extra.astype(BF16)], axis=1)


def tile_kernel(own, other, right, tile, sums, right_ext, total):
    step = pl.program_id(0)
    count, points = right.shape[0], right.shape[1]
    width = count * points

    @pl.when(step == 0)
    def _():
        right_ext[...] = extended(right[...].reshape(width, FEAT), False)
        total[...] = jnp.zeros_like(total)

    blocks = [ref[g] for ref in (own, other) for g in range(BLOCKS)]
    left = extended(jnp.concatenate([b[:points] for b in blocks], axis=0), True)
    values = jnp.concatenate([b[points:] for b in blocks], axis=1)
    for start in range(0, width, CHUNK):
        at = slice(start, start + CHUNK)
        exponent = lax.dot_general(
            left, right_ext[at, :], (((1,), (1,)), ((), ())), preferred_element_type=F32
        )
        kernel = jnp.exp2(exponent * LOG2E).astype(BF16)
        tile[:, at] = kernel
        total[:, at] += jnp.dot(values, kernel, preferred_element_type=F32)

    @pl.when(step == pl.num_programs(0) - 1)
    def _():
        for k in range(count):
            sums[k] = total[:, k * points : (k + 1) * points]


def tile_and_sums(own, other, right):
    blocks, packed, _ = own.shape
    count, points, _ = right.shape
    rows, width = 2 * BLOCKS * points, count * points
    left_spec = pl.BlockSpec((BLOCKS, packed, FEAT), lambda i: (i, 0, 0))
    return pl.pallas_call(
        tile_kernel,
        grid=(blocks // BLOCKS,),
        in_specs=[left_spec, left_spec, pl.BlockSpec(right.shape, lambda i: (0, 0, 0))],
        out_specs=[
            pl.BlockSpec((rows, width), lambda i: (i, 0)),
            pl.BlockSpec((count, CLASSES, points), lambda i: (0, 0, 0)),
        ],
        out_shape=[
            jax.ShapeDtypeStruct((2 * blocks * points, width), BF16),
            jax.ShapeDtypeStruct((count, CLASSES, points), F32),
        ],
        scratch_shapes=[pltpu.VMEM((width, 2 * FEAT), BF16), pltpu.VMEM((CLASSES, width), F32)],
        compiler_params=pltpu.CompilerParams(vmem_limit_bytes=32 << 20),
        name="tile_and_sums",
    )(own, other, right)


def apply_kernel(own, other, tile, sums, total):
    step = pl.program_id(0)
    count, _, points = sums.shape

    @pl.when(step == 0)
    def _():
        total[...] = jnp.zeros_like(total)

    values = jnp.concatenate([ref[g] for ref in (own, other) for g in range(BLOCKS)], axis=1)
    total[...] += jnp.dot(values, tile[...], preferred_element_type=F32)

    @pl.when(step == pl.num_programs(0) - 1)
    def _():
        for k in range(count):
            sums[k] = total[:, k * points : (k + 1) * points]


def apply_tile(own, other, tile, count):
    blocks, _, points = own.shape
    rows, width = 2 * BLOCKS * points, tile.shape[1]
    left_spec = pl.BlockSpec((BLOCKS, CLASSES, points), lambda i: (i, 0, 0))
    return pl.pallas_call(
        apply_kernel,
        grid=(blocks // BLOCKS,),
        in_specs=[left_spec, left_spec, pl.BlockSpec((rows, width), lambda i: (i, 0))],
        out_specs=pl.BlockSpec((count, CLASSES, points), lambda i: (0, 0, 0)),
        out_shape=jax.ShapeDtypeStruct((count, CLASSES, points), F32),
        scratch_shapes=[pltpu.VMEM((CLASSES, width), F32)],
        compiler_params=pltpu.CompilerParams(vmem_limit_bytes=32 << 20),
        name="apply_tile",
    )(own, other, tile)


def on_device(rows, cols, points, labels, coefficients):
    total_points = points.shape[0] * rows * cols
    logit_scale = 16.0 / math.sqrt(total_points)
    in_z, in_plane = z_groups(cols), plane_groups(rows, cols)
    zs, planes = len(in_z[0]), len(in_plane[0])

    def along_z(value):
        copies = jnp.broadcast_to(value[None], (zs, *value.shape))
        return lax.all_to_all(copies, "col", 0, 0, tiled=True, axis_index_groups=in_z)

    def in_the_plane(parts):
        return lax.all_to_all(
            parts, ("row", "col"), 0, 0, tiled=True, axis_index_groups=in_plane
        )

    current = coefficients.T
    near = points.astype(BF16)
    own = along_z(jnp.concatenate([near, current.astype(BF16)], axis=0))
    other = other_core(own, cols)
    right = in_the_plane(jnp.broadcast_to(near[None], (planes, *near.shape)))
    tile, sums = tile_and_sums(own, other, right)
    logits = logit_scale * in_the_plane(sums).sum(axis=0)
    probabilities = jax.nn.softmax(logits, axis=0)
    classes = jnp.arange(CLASSES, dtype=jnp.int32)
    onehot = (labels[None, :] == classes[:, None]).astype(F32)
    residual = logit_scale * (probabilities - onehot)
    own = along_z(residual.astype(BF16))
    sums = apply_tile(own, other_core(own, cols), tile, planes)
    current = current - in_the_plane(sums).sum(axis=0)
    return current.T, probabilities.T


def solution(mesh):
    rows, cols = mesh.shape["row"], mesh.shape["col"]
    return jax.shard_map(
        functools.partial(on_device, rows, cols),
        mesh=mesh,
        in_specs=(P(("row", "col"), None), P(("row", "col")), P(("row", "col"), None)),
        out_specs=(P(("row", "col"), None), P(("row", "col"), None)),
        check_vma=False,
    )
```

```python
import functools
import math

import jax
import jax.numpy as jnp
from jax import lax
from jax.experimental import pallas as pl
from jax.experimental.pallas import tpu as pltpu
from jax.sharding import PartitionSpec as P


FEAT = 128
CLASSES = 64
LOG2E = math.log2(math.e)
ROWS = 1024
CHUNK = 512
BF16 = jnp.bfloat16
F32 = jnp.float32


def z_groups(cols):
    return [[z * 4 + rest for z in range(cols // 4)] for rest in range(4)]


def plane_groups(rows, cols):
    return [
        [row * cols + z * 4 + y_hi * 2 + core for row in range(rows) for y_hi in range(2)]
        for z in range(cols // 4)
        for core in range(2)
    ]


def other_core(value, cols):
    return lax.ppermute(value, "col", [(col, col ^ 1) for col in range(cols)])


def extended(block, left):
    rows = block.shape[0]
    wide = block.astype(F32)
    square = jnp.sum(wide * wide, axis=1, keepdims=True) * (-1.0 / FEAT)
    first = square.astype(BF16).astype(F32)
    second = square - first
    lane = lax.broadcasted_iota(jnp.int32, (rows, FEAT), 1)
    at = 0 if left else 2
    ones = 2 - at
    extra = jnp.where((lane >= ones) & (lane < ones + 2), 1.0, 0.0)
    extra = jnp.where(lane == at, first, extra)
    extra = jnp.where(lane == at + 1, second, extra)
    scaled = block * jnp.asarray(2.0 / FEAT, BF16) if left else block
    return jnp.concatenate([scaled, extra.astype(BF16)], axis=1)


def build_tile(packed, right_ext, tile):
    points, width = packed.shape[1] - CLASSES, tile.shape[1]
    per_step = ROWS // points
    for step in range(packed.shape[0] // per_step):
        blocks = range(step * per_step, (step + 1) * per_step)
        left = jnp.concatenate([extended(packed[g, :points, :], True) for g in blocks], axis=0)
        for start in range(0, width, CHUNK):
            exponent = lax.dot_general(
                left,
                right_ext[start : start + CHUNK, :],
                (((1,), (1,)), ((), ())),
                preferred_element_type=F32,
            )
            tile[step * ROWS : (step + 1) * ROWS, start : start + CHUNK] = jnp.exp2(
                exponent * LOG2E
            ).astype(BF16)


def side_by_side(values):
    return jnp.concatenate([values[g] for g in range(values.shape[0])], axis=1)


def own_kernel(own, right, tile, right_ext):
    count, points, _ = right.shape
    for k in range(count):
        right_ext[k * points : (k + 1) * points, :] = extended(right[k], False)
    build_tile(own, right_ext, tile)


def other_kernel(own, own_tile, other, right_ext, tile, sums):
    count, _, points = sums.shape
    build_tile(other, right_ext, tile)
    rows = other.shape[1] - CLASSES
    total = jnp.dot(
        side_by_side(own[:, rows:, :]), own_tile[...], preferred_element_type=F32
    ) + jnp.dot(side_by_side(other[:, rows:, :]), tile[...], preferred_element_type=F32)
    for k in range(count):
        sums[k] = total[:, k * points : (k + 1) * points]


def tile_from_own(own, right):
    blocks, _, _ = own.shape
    count, points, _ = right.shape
    rows, width = blocks * points, count * points
    return pl.pallas_call(
        own_kernel,
        out_shape=[
            jax.ShapeDtypeStruct((rows, width), BF16),
            jax.ShapeDtypeStruct((width, 2 * FEAT), BF16),
        ],
        compiler_params=pltpu.CompilerParams(vmem_limit_bytes=16 << 20),
        cost_estimate=pl.CostEstimate(
            flops=4 * rows * width * FEAT, bytes_accessed=0, transcendentals=rows * width
        ),
        name="tile_from_own",
    )(own, right)


def tile_from_other(own, own_tile, other, right_ext, count):
    rows, width = own_tile.shape
    return pl.pallas_call(
        other_kernel,
        out_shape=[
            jax.ShapeDtypeStruct((rows, width), BF16),
            jax.ShapeDtypeStruct((count, CLASSES, width // count), F32),
        ],
        compiler_params=pltpu.CompilerParams(vmem_limit_bytes=16 << 20),
        name="tile_from_other",
    )(own, own_tile, other, right_ext)


def apply_kernel(own, own_tile, other, other_tile, sums):
    count, _, points = sums.shape
    total = jnp.dot(side_by_side(own), own_tile[...], preferred_element_type=F32) + jnp.dot(
        side_by_side(other), other_tile[...], preferred_element_type=F32
    )
    for k in range(count):
        sums[k] = total[:, k * points : (k + 1) * points]


def apply_tiles(own, own_tile, other, other_tile, count):
    points = own_tile.shape[1] // count
    return pl.pallas_call(
        apply_kernel,
        out_shape=jax.ShapeDtypeStruct((count, CLASSES, points), F32),
        compiler_params=pltpu.CompilerParams(vmem_limit_bytes=16 << 20),
        name="apply_tiles",
    )(own, own_tile, other, other_tile)


def pack_kernel(points, current, labels, packed, near, kept, kept_labels, wide, sems):
    rows = points.shape[0]
    copies = [
        pltpu.make_async_copy(source, target, sems.at[k])
        for k, (source, target) in enumerate(
            ((points, wide), (current, kept), (labels, kept_labels))
        )
    ]
    for copy in copies:
        copy.start()
    copies[0].wait()
    narrow = wide[...].astype(BF16)
    for k in range(near.shape[0]):
        near[k] = narrow
    for k in range(packed.shape[0]):
        packed[k, :rows] = narrow
    copies[1].wait()
    values = kept[...].astype(BF16)
    for k in range(packed.shape[0]):
        packed[k, rows:] = values
    copies[2].wait()


def pack(points, current, labels, zs, planes):
    rows = points.shape[0]
    in_hbm = pl.BlockSpec(memory_space=pltpu.HBM)
    in_vmem = pl.BlockSpec(memory_space=pltpu.VMEM)
    return pl.pallas_call(
        pack_kernel,
        in_specs=[in_hbm] * 3,
        out_specs=[in_vmem] * 4,
        out_shape=[
            jax.ShapeDtypeStruct((zs, rows + CLASSES, FEAT), BF16),
            jax.ShapeDtypeStruct((planes, rows, FEAT), BF16),
            jax.ShapeDtypeStruct(current.shape, F32),
            jax.ShapeDtypeStruct(labels.shape, jnp.int32),
        ],
        scratch_shapes=[pltpu.VMEM(points.shape, F32), pltpu.SemaphoreType.DMA((3,))],
        compiler_params=pltpu.CompilerParams(vmem_limit_bytes=8 << 20),
        name="pack",
    )(*(pltpu.with_memory_space_constraint(v, pltpu.HBM) for v in (points, current, labels)))


def softmax_kernel(logit_scale, parts, labels, residual, probabilities):
    logits = logit_scale * jnp.sum(parts[...], axis=0)
    raised = jnp.exp(logits - jnp.max(logits, axis=0, keepdims=True))
    value = raised / jnp.sum(raised, axis=0, keepdims=True)
    classes = lax.broadcasted_iota(jnp.int32, value.shape, 0)
    onehot = jnp.where(classes == labels[...], 1.0, 0.0)
    change = (logit_scale * (value - onehot)).astype(BF16)
    probabilities[...] = value
    for k in range(residual.shape[0]):
        residual[k] = change


def softmax_and_residual(parts, labels, logit_scale, zs):
    _, classes, points = parts.shape
    return pl.pallas_call(
        functools.partial(softmax_kernel, logit_scale),
        out_shape=[
            jax.ShapeDtypeStruct((zs, classes, points), BF16),
            jax.ShapeDtypeStruct((classes, points), F32),
        ],
        compiler_params=pltpu.CompilerParams(vmem_limit_bytes=8 << 20),
        name="softmax_and_residual",
    )(parts, labels)


def finish_kernel(parts, current, probabilities, new_current, out_probabilities):
    new_current[...] = current[...] - jnp.sum(parts[...], axis=0)
    out_probabilities[...] = probabilities[...]


def finish(parts, current, probabilities):
    shape = jax.ShapeDtypeStruct(current.shape, F32)
    return pl.pallas_call(
        finish_kernel,
        out_shape=[shape, shape],
        compiler_params=pltpu.CompilerParams(vmem_limit_bytes=8 << 20),
        name="finish",
    )(parts, current, probabilities)


def on_device(rows, cols, points, labels, coefficients):
    total_points = points.shape[0] * rows * cols
    logit_scale = 16.0 / math.sqrt(total_points)
    in_z, in_plane = z_groups(cols), plane_groups(rows, cols)
    zs, planes = len(in_z[0]), len(in_plane[0])

    def along_z(parts):
        return lax.all_to_all(parts, "col", 0, 0, tiled=True, axis_index_groups=in_z)

    def in_the_plane(parts):
        return lax.all_to_all(
            parts, ("row", "col"), 0, 0, tiled=True, axis_index_groups=in_plane
        )

    current = coefficients.T
    packed, near, current, labels = pack(points, current, labels[None, :], zs, planes)
    right = in_the_plane(near)
    own = along_z(packed)
    other = other_core(own, cols)
    own_tile, right_ext = tile_from_own(own, right)
    other_tile, sums = tile_from_other(own, own_tile, other, right_ext, planes)
    residual, probabilities = softmax_and_residual(
        in_the_plane(sums), labels, logit_scale, zs
    )
    own = along_z(residual)
    sums = apply_tiles(own, own_tile, other_core(own, cols), other_tile, planes)
    current, probabilities = finish(in_the_plane(sums), current, probabilities)
    return current.T, probabilities.T


def solution(mesh):
    rows, cols = mesh.shape["row"], mesh.shape["col"]
    return jax.shard_map(
        functools.partial(on_device, rows, cols),
        mesh=mesh,
        in_specs=(P(("row", "col"), None), P(("row", "col")), P(("row", "col"), None)),
        out_specs=(P(("row", "col"), None), P(("row", "col"), None)),
        check_vma=False,
    )
```

```python
import functools
import math

import jax
import jax.numpy as jnp
from jax import lax
from jax.experimental import pallas as pl
from jax.experimental.pallas import tpu as pltpu
from jax.sharding import PartitionSpec as P


FEAT = 128
CLASSES = 64
LOG2E = math.log2(math.e)
CHUNK = 512
BF16 = jnp.bfloat16
F32 = jnp.float32


def z_groups(cols):
    return [[z * 4 + rest for z in range(cols // 4)] for rest in range(4)]


def facing(row):
    return (row + 4) % 8


def row_block_groups(rows, cols):
    return [
        [
            (facing(row) if y_hi else row) * cols + z * 4 + y_hi * 2 + core
            for y_hi in range(2)
            for z in range(cols // 4)
        ]
        for row in range(rows)
        for core in range(2)
    ]


def other_core(value, cols):
    return lax.ppermute(value, "col", [(col, col ^ 1) for col in range(cols)])


def facing_y(value, rows, cols):
    pairs = [
        (row * cols + col, facing(row) * cols + (col ^ 2))
        for row in range(rows)
        for col in range(cols)
    ]
    return lax.ppermute(value, ("row", "col"), pairs)


def extended(block, left):
    rows = block.shape[0]
    wide = block.astype(F32)
    square = jnp.sum(wide * wide, axis=1, keepdims=True) * (-1.0 / FEAT)
    first = square.astype(BF16).astype(F32)
    second = square - first
    lane = lax.broadcasted_iota(jnp.int32, (rows, FEAT), 1)
    at = 0 if left else 2
    ones = 2 - at
    extra = jnp.where((lane >= ones) & (lane < ones + 2), 1.0, 0.0)
    extra = jnp.where(lane == at, first, extra)
    extra = jnp.where(lane == at + 1, second, extra)
    scaled = block * jnp.asarray(2.0 / FEAT, BF16) if left else block
    return jnp.concatenate([scaled, extra.astype(BF16)], axis=1)


def side_by_side(values):
    return jnp.concatenate([values[g] for g in range(values.shape[0])], axis=1)


def build_part(packed, right_ext, tile):
    points = packed.shape[1] - CLASSES
    left = jnp.concatenate(
        [extended(packed[g, :points, :], True) for g in range(packed.shape[0])], axis=0
    )
    for start in range(0, tile.shape[1], CHUNK):
        exponent = lax.dot_general(
            left,
            right_ext[start : start + CHUNK, :],
            (((1,), (1,)), ((), ())),
            preferred_element_type=F32,
        )
        tile[:, start : start + CHUNK] = jnp.exp2(exponent * LOG2E).astype(BF16)
    return jnp.dot(
        side_by_side(packed[:, points:, :]), tile[...], preferred_element_type=F32
    )


def write_blocks(total, sums):
    count, _, points = sums.shape
    for k in range(count):
        sums[k] = total[:, k * points : (k + 1) * points]


def first_kernel(packed, right, tile, right_ext, total):
    count, points, _ = right.shape
    for k in range(count):
        right_ext[k * points : (k + 1) * points, :] = extended(right[k], False)
    total[...] = build_part(packed, right_ext, tile)


def next_kernel(packed, right_ext, before, tile, total):
    total[...] = before[...] + build_part(packed, right_ext, tile)


def last_kernel(packed, right_ext, before, tile, sums):
    write_blocks(before[...] + build_part(packed, right_ext, tile), sums)


def tile_part(body, out_shape, rows, width, *operands):
    return pl.pallas_call(
        body,
        out_shape=[jax.ShapeDtypeStruct((rows, width), BF16), *out_shape],
        compiler_params=pltpu.CompilerParams(vmem_limit_bytes=16 << 20),
        cost_estimate=pl.CostEstimate(
            flops=4 * rows * width * FEAT, bytes_accessed=0, transcendentals=rows * width
        ),
    )(*operands)


def apply_kernel(own, other, own_near, own_far, other_near, other_far, sums):
    near = (lax.axis_index("col") // 2) % 2
    total = jnp.dot(side_by_side(own[near]), own_near[...], preferred_element_type=F32)
    total += jnp.dot(side_by_side(own[1 - near]), own_far[...], preferred_element_type=F32)
    total += jnp.dot(side_by_side(other[near]), other_near[...], preferred_element_type=F32)
    total += jnp.dot(side_by_side(other[1 - near]), other_far[...], preferred_element_type=F32)
    write_blocks(total, sums)


def apply_tile(own, other, tile, count):
    points = tile[0].shape[1] // count
    return pl.pallas_call(
        apply_kernel,
        out_shape=jax.ShapeDtypeStruct((count, CLASSES, points), F32),
        compiler_params=pltpu.CompilerParams(vmem_limit_bytes=16 << 20),
        name="apply_tile",
    )(own, other, *tile)


def pack_kernel(points, current, labels, packed, near, kept, kept_labels, wide, sems):
    rows = points.shape[0]
    copies = [
        pltpu.make_async_copy(source, target, sems.at[k])
        for k, (source, target) in enumerate(
            ((points, wide), (current, kept), (labels, kept_labels))
        )
    ]
    for copy in copies:
        copy.start()
    copies[0].wait()
    narrow = wide[...].astype(BF16)
    for k in range(near.shape[0]):
        near[k] = narrow
    for k in range(packed.shape[0]):
        packed[k, :rows] = narrow
    copies[1].wait()
    values = kept[...].astype(BF16)
    for k in range(packed.shape[0]):
        packed[k, rows:] = values
    copies[2].wait()


def pack(points, current, labels, zs, rights):
    rows = points.shape[0]
    in_hbm = pl.BlockSpec(memory_space=pltpu.HBM)
    in_vmem = pl.BlockSpec(memory_space=pltpu.VMEM)
    return pl.pallas_call(
        pack_kernel,
        in_specs=[in_hbm] * 3,
        out_specs=[in_vmem] * 4,
        out_shape=[
            jax.ShapeDtypeStruct((zs, rows + CLASSES, FEAT), BF16),
            jax.ShapeDtypeStruct((rights, rows, FEAT), BF16),
            jax.ShapeDtypeStruct(current.shape, F32),
            jax.ShapeDtypeStruct(labels.shape, jnp.int32),
        ],
        scratch_shapes=[pltpu.VMEM(points.shape, F32), pltpu.SemaphoreType.DMA((3,))],
        compiler_params=pltpu.CompilerParams(vmem_limit_bytes=8 << 20),
        name="pack",
    )(*(pltpu.with_memory_space_constraint(v, pltpu.HBM) for v in (points, current, labels)))


def softmax_kernel(logit_scale, parts, labels, residual, probabilities):
    logits = logit_scale * jnp.sum(parts[...], axis=0)
    raised = jnp.exp(logits - jnp.max(logits, axis=0, keepdims=True))
    value = raised / jnp.sum(raised, axis=0, keepdims=True)
    classes = lax.broadcasted_iota(jnp.int32, value.shape, 0)
    onehot = jnp.where(classes == labels[...], 1.0, 0.0)
    change = (logit_scale * (value - onehot)).astype(BF16)
    probabilities[...] = value
    for k in range(residual.shape[0]):
        residual[k] = change


def softmax_and_residual(parts, labels, logit_scale, zs):
    _, classes, points = parts.shape
    return pl.pallas_call(
        functools.partial(softmax_kernel, logit_scale),
        out_shape=[
            jax.ShapeDtypeStruct((zs, classes, points), BF16),
            jax.ShapeDtypeStruct((classes, points), F32),
        ],
        compiler_params=pltpu.CompilerParams(vmem_limit_bytes=8 << 20),
        name="softmax_and_residual",
    )(parts, labels)


def finish_kernel(parts, current, probabilities, new_current, out_probabilities):
    new_current[...] = current[...] - jnp.sum(parts[...], axis=0)
    out_probabilities[...] = probabilities[...]


def finish(parts, current, probabilities):
    shape = jax.ShapeDtypeStruct(current.shape, F32)
    return pl.pallas_call(
        finish_kernel,
        out_shape=[shape, shape],
        compiler_params=pltpu.CompilerParams(vmem_limit_bytes=8 << 20),
        name="finish",
    )(parts, current, probabilities)


def on_device(rows, cols, points, labels, coefficients):
    count = points.shape[0]
    logit_scale = 16.0 / math.sqrt(count * rows * cols)
    zs = cols // 4

    def over_rows(parts):
        return lax.all_to_all(parts, "row", 0, 0, tiled=True)

    current = coefficients.T
    packed, near, current, labels = pack(points, current, labels[None, :], zs, rows)
    own_near = lax.all_to_all(
        packed, "col", 0, 0, tiled=True, axis_index_groups=z_groups(cols)
    )
    own_far = facing_y(own_near, rows, cols)
    other_near = other_core(own_near, cols)
    right = over_rows(near)
    high, width = zs * count, rows * count
    total = jax.ShapeDtypeStruct((CLASSES, width), F32)
    right_ext = jax.ShapeDtypeStruct((width, 2 * FEAT), BF16)
    own_near_tile, right_ext, total = tile_part(
        first_kernel, [right_ext, total], high, width, own_near, right
    )
    other_near_tile, total = tile_part(
        next_kernel, [total], high, width, other_near, right_ext, total
    )
    other_far = other_core(own_far, cols)
    own_far_tile, total = tile_part(next_kernel, [total], high, width, own_far, right_ext, total)
    sums = jax.ShapeDtypeStruct((rows, CLASSES, count), F32)
    other_far_tile, sums = tile_part(last_kernel, [sums], high, width, other_far, right_ext, total)
    tile = own_near_tile, own_far_tile, other_near_tile, other_far_tile
    residual, probabilities = softmax_and_residual(
        over_rows(sums), labels, logit_scale, 2 * zs
    )
    own = lax.all_to_all(
        residual,
        ("row", "col"),
        0,
        0,
        tiled=True,
        axis_index_groups=row_block_groups(rows, cols),
    ).reshape(2, zs, CLASSES, count)
    sums = apply_tile(own, other_core(own, cols), tile, rows)
    current, probabilities = finish(over_rows(sums), current, probabilities)
    return current.T, probabilities.T


def solution(mesh):
    rows, cols = mesh.shape["row"], mesh.shape["col"]
    return jax.shard_map(
        functools.partial(on_device, rows, cols),
        mesh=mesh,
        in_specs=(P(("row", "col"), None), P(("row", "col")), P(("row", "col"), None)),
        out_specs=(P(("row", "col"), None), P(("row", "col"), None)),
        check_vma=False,
    )
```

```python
import functools
import math

import jax
import jax.numpy as jnp
from jax import lax
from jax.experimental import pallas as pl
from jax.experimental.pallas import tpu as pltpu
from jax.sharding import PartitionSpec as P


FEAT = 128
CLASSES = 64
LOG2E = math.log2(math.e)
CHUNK = 512
BF16 = jnp.bfloat16
F32 = jnp.float32


def z_groups(cols):
    return [[z * 4 + rest for z in range(cols // 4)] for rest in range(4)]


def facing(row):
    return (row + 4) % 8


def row_block_groups(rows, cols):
    return [
        [
            (facing(row) if y_hi else row) * cols + z * 4 + y_hi * 2 + core
            for y_hi in range(2)
            for z in range(cols // 4)
        ]
        for row in range(rows)
        for core in range(2)
    ]


def other_core(value, cols):
    return lax.ppermute(value, "col", [(col, col ^ 1) for col in range(cols)])


def facing_y(value, rows, cols):
    pairs = [
        (row * cols + col, facing(row) * cols + (col ^ 2))
        for row in range(rows)
        for col in range(cols)
    ]
    return lax.ppermute(value, ("row", "col"), pairs)


def extended(block, left):
    rows = block.shape[0]
    wide = block.astype(F32)
    square = jnp.sum(wide * wide, axis=1, keepdims=True) * (-1.0 / FEAT)
    first = square.astype(BF16).astype(F32)
    second = square - first
    lane = lax.broadcasted_iota(jnp.int32, (rows, FEAT), 1)
    at = 0 if left else 2
    ones = 2 - at
    extra = jnp.where((lane >= ones) & (lane < ones + 2), 1.0, 0.0)
    extra = jnp.where(lane == at, first, extra)
    extra = jnp.where(lane == at + 1, second, extra)
    scaled = block * jnp.asarray(2.0 / FEAT, BF16) if left else block
    return jnp.concatenate([scaled, extra.astype(BF16)], axis=1)


def side_by_side(values):
    return jnp.concatenate([values[g] for g in range(values.shape[0])], axis=1)


def build_part(packed, right_ext, tile):
    points = packed.shape[1] - CLASSES
    left = jnp.concatenate(
        [extended(packed[g, :points, :], True) for g in range(packed.shape[0])], axis=0
    )
    for start in range(0, tile.shape[1], CHUNK):
        exponent = lax.dot_general(
            left,
            right_ext[start : start + CHUNK, :],
            (((1,), (1,)), ((), ())),
            preferred_element_type=F32,
        )
        tile[:, start : start + CHUNK] = jnp.exp2(exponent * LOG2E).astype(BF16)
    return jnp.dot(
        side_by_side(packed[:, points:, :]), tile[...], preferred_element_type=F32
    )


def write_blocks(total, sums):
    count, _, points = sums.shape
    for k in range(count):
        sums[k] = total[:, k * points : (k + 1) * points]


def first_kernel(packed, right, tile, right_ext, total):
    count, points, _ = right.shape
    for k in range(count):
        right_ext[k * points : (k + 1) * points, :] = extended(right[k], False)
    total[...] = build_part(packed, right_ext, tile)


def next_kernel(packed, right_ext, before, tile, total):
    total[...] = before[...] + build_part(packed, right_ext, tile)


def last_kernel(packed, right_ext, before, tile, sums):
    write_blocks(before[...] + build_part(packed, right_ext, tile), sums)


def tile_part(body, out_shape, rows, width, *operands):
    return pl.pallas_call(
        body,
        out_shape=[jax.ShapeDtypeStruct((rows, width), BF16), *out_shape],
        compiler_params=pltpu.CompilerParams(vmem_limit_bytes=16 << 20),
        cost_estimate=pl.CostEstimate(
            flops=4 * rows * width * FEAT, bytes_accessed=0, transcendentals=rows * width
        ),
    )(*operands)


def product(values, near_tile, far_tile):
    near = (lax.axis_index("col") // 2) % 2
    return jnp.dot(
        side_by_side(values[near]), near_tile[...], preferred_element_type=F32
    ) + jnp.dot(side_by_side(values[1 - near]), far_tile[...], preferred_element_type=F32)


def apply_own_kernel(values, near_tile, far_tile, total):
    total[...] = product(values, near_tile, far_tile)


def apply_other_kernel(values, near_tile, far_tile, before, sums):
    write_blocks(before[...] + product(values, near_tile, far_tile), sums)


def apply_part(body, out_shape, *operands):
    rows, width = operands[1].shape
    return pl.pallas_call(
        body,
        out_shape=out_shape,
        compiler_params=pltpu.CompilerParams(vmem_limit_bytes=16 << 20),
        cost_estimate=pl.CostEstimate(
            flops=4 * rows * width * CLASSES, bytes_accessed=0, transcendentals=0
        ),
    )(*operands)


def pack_kernel(points, current, labels, packed, near, kept, kept_labels, wide, sems):
    rows = points.shape[0]
    copies = [
        pltpu.make_async_copy(source, target, sems.at[k])
        for k, (source, target) in enumerate(
            ((points, wide), (current, kept), (labels, kept_labels))
        )
    ]
    for copy in copies:
        copy.start()
    copies[0].wait()
    narrow = wide[...].astype(BF16)
    for k in range(near.shape[0]):
        near[k] = narrow
    for k in range(packed.shape[0]):
        packed[k, :rows] = narrow
    copies[1].wait()
    values = kept[...].astype(BF16)
    for k in range(packed.shape[0]):
        packed[k, rows:] = values
    copies[2].wait()


def pack(points, current, labels, zs, rights):
    rows = points.shape[0]
    in_hbm = pl.BlockSpec(memory_space=pltpu.HBM)
    in_vmem = pl.BlockSpec(memory_space=pltpu.VMEM)
    return pl.pallas_call(
        pack_kernel,
        in_specs=[in_hbm] * 3,
        out_specs=[in_vmem] * 4,
        out_shape=[
            jax.ShapeDtypeStruct((zs, rows + CLASSES, FEAT), BF16),
            jax.ShapeDtypeStruct((rights, rows, FEAT), BF16),
            jax.ShapeDtypeStruct(current.shape, F32),
            jax.ShapeDtypeStruct(labels.shape, jnp.int32),
        ],
        scratch_shapes=[pltpu.VMEM(points.shape, F32), pltpu.SemaphoreType.DMA((3,))],
        compiler_params=pltpu.CompilerParams(vmem_limit_bytes=8 << 20),
        name="pack",
    )(*(pltpu.with_memory_space_constraint(v, pltpu.HBM) for v in (points, current, labels)))


def softmax_kernel(logit_scale, parts, labels, residual, probabilities):
    logits = logit_scale * jnp.sum(parts[...], axis=0)
    raised = jnp.exp(logits - jnp.max(logits, axis=0, keepdims=True))
    value = raised / jnp.sum(raised, axis=0, keepdims=True)
    classes = lax.broadcasted_iota(jnp.int32, value.shape, 0)
    onehot = jnp.where(classes == labels[...], 1.0, 0.0)
    change = (logit_scale * (value - onehot)).astype(BF16)
    probabilities[...] = value
    for k in range(residual.shape[0]):
        residual[k] = change


def softmax_and_residual(parts, labels, logit_scale, zs):
    _, classes, points = parts.shape
    return pl.pallas_call(
        functools.partial(softmax_kernel, logit_scale),
        out_shape=[
            jax.ShapeDtypeStruct((zs, classes, points), BF16),
            jax.ShapeDtypeStruct((classes, points), F32),
        ],
        compiler_params=pltpu.CompilerParams(vmem_limit_bytes=8 << 20),
        name="softmax_and_residual",
    )(parts, labels)


def finish_kernel(parts, current, probabilities, new_current, out_probabilities):
    new_current[...] = current[...] - jnp.sum(parts[...], axis=0)
    out_probabilities[...] = probabilities[...]


def finish(parts, current, probabilities):
    shape = jax.ShapeDtypeStruct(current.shape, F32)
    return pl.pallas_call(
        finish_kernel,
        out_shape=[shape, shape],
        compiler_params=pltpu.CompilerParams(vmem_limit_bytes=8 << 20),
        name="finish",
    )(parts, current, probabilities)


def on_device(rows, cols, points, labels, coefficients):
    count = points.shape[0]
    logit_scale = 16.0 / math.sqrt(count * rows * cols)
    zs = cols // 4

    def over_rows(parts):
        return lax.all_to_all(parts, "row", 0, 0, tiled=True)

    current = coefficients.T
    packed, near, current, labels = pack(points, current, labels[None, :], zs, rows)
    own_near = lax.all_to_all(
        packed, "col", 0, 0, tiled=True, axis_index_groups=z_groups(cols)
    )
    own_far = facing_y(own_near, rows, cols)
    other_near = other_core(own_near, cols)
    right = over_rows(near)
    high, width = zs * count, rows * count
    total_shape = jax.ShapeDtypeStruct((CLASSES, width), F32)
    right_ext = jax.ShapeDtypeStruct((width, 2 * FEAT), BF16)
    own_near_tile, right_ext, total = tile_part(
        first_kernel, [right_ext, total_shape], high, width, own_near, right
    )
    other_near_tile, total = tile_part(
        next_kernel, [total_shape], high, width, other_near, right_ext, total
    )
    other_far = other_core(own_far, cols)
    own_far_tile, total = tile_part(
        next_kernel, [total_shape], high, width, own_far, right_ext, total
    )
    sums_shape = jax.ShapeDtypeStruct((rows, CLASSES, count), F32)
    other_far_tile, sums = tile_part(
        last_kernel, [sums_shape], high, width, other_far, right_ext, total
    )
    residual, probabilities = softmax_and_residual(
        over_rows(sums), labels, logit_scale, 2 * zs
    )
    own = lax.all_to_all(
        residual,
        ("row", "col"),
        0,
        0,
        tiled=True,
        axis_index_groups=row_block_groups(rows, cols),
    ).reshape(2, zs, CLASSES, count)
    other = other_core(own, cols)
    total = apply_part(apply_own_kernel, total_shape, own, own_near_tile, own_far_tile)
    sums = apply_part(apply_other_kernel, sums_shape, other, other_near_tile, other_far_tile, total)
    current, probabilities = finish(over_rows(sums), current, probabilities)
    return current.T, probabilities.T


def solution(mesh):
    rows, cols = mesh.shape["row"], mesh.shape["col"]
    return jax.shard_map(
        functools.partial(on_device, rows, cols),
        mesh=mesh,
        in_specs=(P(("row", "col"), None), P(("row", "col")), P(("row", "col"), None)),
        out_specs=(P(("row", "col"), None), P(("row", "col"), None)),
        check_vma=False,
    )
```

```python
import functools
import math

import jax
import jax.numpy as jnp
from jax import lax
from jax.experimental import pallas as pl
from jax.experimental.pallas import tpu as pltpu
from jax.sharding import PartitionSpec as P


FEAT = 128
CLASSES = 64
LOG2E = math.log2(math.e)
CHUNK = 512
BF16 = jnp.bfloat16
F32 = jnp.float32


def z_groups(cols):
    return [[z * 4 + rest for z in range(cols // 4)] for rest in range(4)]


def facing(row):
    return (row + 4) % 8


def row_block_groups(rows, cols):
    return [
        [
            (facing(row) if y_hi else row) * cols + z * 4 + y_hi * 2 + core
            for y_hi in range(2)
            for z in range(cols // 4)
        ]
        for row in range(rows)
        for core in range(2)
    ]


def other_core(value, cols):
    return lax.ppermute(value, "col", [(col, col ^ 1) for col in range(cols)])


def facing_y(value, rows, cols):
    pairs = [
        (row * cols + col, facing(row) * cols + (col ^ 2))
        for row in range(rows)
        for col in range(cols)
    ]
    return lax.ppermute(value, ("row", "col"), pairs)


def extended(block, left):
    rows = block.shape[0]
    wide = block.astype(F32)
    square = jnp.sum(wide * wide, axis=1, keepdims=True) * (-1.0 / FEAT)
    first = square.astype(BF16).astype(F32)
    second = square - first
    lane = lax.broadcasted_iota(jnp.int32, (rows, FEAT), 1)
    at = 0 if left else 2
    ones = 2 - at
    extra = jnp.where((lane >= ones) & (lane < ones + 2), 1.0, 0.0)
    extra = jnp.where(lane == at, first, extra)
    extra = jnp.where(lane == at + 1, second, extra)
    scaled = block * jnp.asarray(2.0 / FEAT, BF16) if left else block
    return jnp.concatenate([scaled, extra.astype(BF16)], axis=1)


def side_by_side(values):
    return jnp.concatenate([values[g] for g in range(values.shape[0])], axis=1)


def build_parts(parts, right_ext, tiles, left_ext):
    points = parts[0].shape[1] - CLASSES
    blocks, width = parts[0].shape[0], tiles[0].shape[1]

    def extend(part, block):
        left_ext[part, block * points : (block + 1) * points, :] = extended(
            parts[part][block, :points, :], True
        )

    for block in range(blocks):
        extend(0, block)
    total = None
    chunks = width // CHUNK
    for part, tile in enumerate(tiles):
        for chunk in range(chunks):
            at = slice(chunk * CHUNK, (chunk + 1) * CHUNK)
            exponent = lax.dot_general(
                left_ext[part],
                right_ext[at, :],
                (((1,), (1,)), ((), ())),
                preferred_element_type=F32,
            )
            tile[:, at] = jnp.exp2(exponent * LOG2E).astype(BF16)
            if part + 1 < len(tiles):
                for block in range(chunk * blocks // chunks, (chunk + 1) * blocks // chunks):
                    extend(part + 1, block)
        values = side_by_side(parts[part][:, points:, :])
        added = jnp.dot(values, tile[...], preferred_element_type=F32)
        total = added if total is None else total + added
    return total


def write_blocks(total, sums):
    count, _, points = sums.shape
    for k in range(count):
        sums[k] = total[:, k * points : (k + 1) * points]


def own_kernel(near, far, right, near_tile, far_tile, right_ext, total, left_ext):
    count, points, _ = right.shape
    for k in range(count):
        right_ext[k * points : (k + 1) * points, :] = extended(right[k], False)
    total[...] = build_parts((near, far), right_ext, (near_tile, far_tile), left_ext)


def other_kernel(near, far, right_ext, before, near_tile, far_tile, sums, left_ext):
    added = build_parts((near, far), right_ext, (near_tile, far_tile), left_ext)
    write_blocks(before[...] + added, sums)


def tile_parts(body, out_shape, rows, width, *operands):
    part = jax.ShapeDtypeStruct((rows, width), BF16)
    return pl.pallas_call(
        body,
        out_shape=[part, part, *out_shape],
        scratch_shapes=[pltpu.VMEM((2, rows, 2 * FEAT), BF16)],
        compiler_params=pltpu.CompilerParams(vmem_limit_bytes=16 << 20),
        cost_estimate=pl.CostEstimate(
            flops=8 * rows * width * FEAT, bytes_accessed=0, transcendentals=2 * rows * width
        ),
    )(*operands)


def product(values, near_tile, far_tile):
    near = (lax.axis_index("col") // 2) % 2
    return jnp.dot(
        side_by_side(values[near]), near_tile[...], preferred_element_type=F32
    ) + jnp.dot(side_by_side(values[1 - near]), far_tile[...], preferred_element_type=F32)


def apply_own_kernel(values, near_tile, far_tile, total):
    total[...] = product(values, near_tile, far_tile)


def apply_other_kernel(values, near_tile, far_tile, before, sums):
    write_blocks(before[...] + product(values, near_tile, far_tile), sums)


def apply_part(body, out_shape, *operands):
    rows, width = operands[1].shape
    return pl.pallas_call(
        body,
        out_shape=out_shape,
        compiler_params=pltpu.CompilerParams(vmem_limit_bytes=16 << 20),
        cost_estimate=pl.CostEstimate(
            flops=4 * rows * width * CLASSES, bytes_accessed=0, transcendentals=0
        ),
    )(*operands)


def pack_kernel(points, current, labels, packed, near, kept, kept_labels, wide, sems):
    rows = points.shape[0]
    copies = [
        pltpu.make_async_copy(source, target, sems.at[k])
        for k, (source, target) in enumerate(
            ((points, wide), (current, kept), (labels, kept_labels))
        )
    ]
    for copy in copies:
        copy.start()
    copies[0].wait()
    narrow = wide[...].astype(BF16)
    for k in range(near.shape[0]):
        near[k] = narrow
    for k in range(packed.shape[0]):
        packed[k, :rows] = narrow
    copies[1].wait()
    values = kept[...].astype(BF16)
    for k in range(packed.shape[0]):
        packed[k, rows:] = values
    copies[2].wait()


def pack(points, current, labels, zs, rights):
    rows = points.shape[0]
    in_hbm = pl.BlockSpec(memory_space=pltpu.HBM)
    in_vmem = pl.BlockSpec(memory_space=pltpu.VMEM)
    return pl.pallas_call(
        pack_kernel,
        in_specs=[in_hbm] * 3,
        out_specs=[in_vmem] * 4,
        out_shape=[
            jax.ShapeDtypeStruct((zs, rows + CLASSES, FEAT), BF16),
            jax.ShapeDtypeStruct((rights, rows, FEAT), BF16),
            jax.ShapeDtypeStruct(current.shape, F32),
            jax.ShapeDtypeStruct(labels.shape, jnp.int32),
        ],
        scratch_shapes=[pltpu.VMEM(points.shape, F32), pltpu.SemaphoreType.DMA((3,))],
        compiler_params=pltpu.CompilerParams(vmem_limit_bytes=8 << 20),
        name="pack",
    )(*(pltpu.with_memory_space_constraint(v, pltpu.HBM) for v in (points, current, labels)))


def softmax_kernel(logit_scale, parts, labels, residual, probabilities):
    logits = logit_scale * jnp.sum(parts[...], axis=0)
    raised = jnp.exp(logits - jnp.max(logits, axis=0, keepdims=True))
    value = raised / jnp.sum(raised, axis=0, keepdims=True)
    classes = lax.broadcasted_iota(jnp.int32, value.shape, 0)
    onehot = jnp.where(classes == labels[...], 1.0, 0.0)
    change = (logit_scale * (value - onehot)).astype(BF16)
    probabilities[...] = value
    for k in range(residual.shape[0]):
        residual[k] = change


def softmax_and_residual(parts, labels, logit_scale, zs):
    _, classes, points = parts.shape
    return pl.pallas_call(
        functools.partial(softmax_kernel, logit_scale),
        out_shape=[
            jax.ShapeDtypeStruct((zs, classes, points), BF16),
            jax.ShapeDtypeStruct((classes, points), F32),
        ],
        compiler_params=pltpu.CompilerParams(vmem_limit_bytes=8 << 20),
        name="softmax_and_residual",
    )(parts, labels)


def finish_kernel(parts, current, probabilities, new_current, out_probabilities):
    new_current[...] = current[...] - jnp.sum(parts[...], axis=0)
    out_probabilities[...] = probabilities[...]


def finish(parts, current, probabilities):
    shape = jax.ShapeDtypeStruct(current.shape, F32)
    return pl.pallas_call(
        finish_kernel,
        out_shape=[shape, shape],
        compiler_params=pltpu.CompilerParams(vmem_limit_bytes=8 << 20),
        name="finish",
    )(parts, current, probabilities)


def on_device(rows, cols, points, labels, coefficients):
    count = points.shape[0]
    logit_scale = 16.0 / math.sqrt(count * rows * cols)
    zs = cols // 4

    def over_rows(parts):
        return lax.all_to_all(parts, "row", 0, 0, tiled=True)

    current = coefficients.T
    packed, near, current, labels = pack(points, current, labels[None, :], zs, rows)
    own_near = lax.all_to_all(
        packed, "col", 0, 0, tiled=True, axis_index_groups=z_groups(cols)
    )
    own_far = facing_y(own_near, rows, cols)
    other_near = other_core(own_near, cols)
    right = over_rows(near)
    high, width = zs * count, rows * count
    total_shape = jax.ShapeDtypeStruct((CLASSES, width), F32)
    right_ext = jax.ShapeDtypeStruct((width, 2 * FEAT), BF16)
    other_far = other_core(own_far, cols)
    own_near_tile, own_far_tile, right_ext, total = tile_parts(
        own_kernel, [right_ext, total_shape], high, width, own_near, own_far, right
    )
    sums_shape = jax.ShapeDtypeStruct((rows, CLASSES, count), F32)
    other_near_tile, other_far_tile, sums = tile_parts(
        other_kernel, [sums_shape], high, width, other_near, other_far, right_ext, total
    )
    residual, probabilities = softmax_and_residual(
        over_rows(sums), labels, logit_scale, 2 * zs
    )
    own = lax.all_to_all(
        residual,
        ("row", "col"),
        0,
        0,
        tiled=True,
        axis_index_groups=row_block_groups(rows, cols),
    ).reshape(2, zs, CLASSES, count)
    other = other_core(own, cols)
    total = apply_part(apply_own_kernel, total_shape, own, own_near_tile, own_far_tile)
    sums = apply_part(
        apply_other_kernel, sums_shape, other, other_near_tile, other_far_tile, total
    )
    current, probabilities = finish(over_rows(sums), current, probabilities)
    return current.T, probabilities.T


def solution(mesh):
    rows, cols = mesh.shape["row"], mesh.shape["col"]
    return jax.shard_map(
        functools.partial(on_device, rows, cols),
        mesh=mesh,
        in_specs=(P(("row", "col"), None), P(("row", "col")), P(("row", "col"), None)),
        out_specs=(P(("row", "col"), None), P(("row", "col"), None)),
        check_vma=False,
    )
```
